256 devices in a mesh: ka: 16 (over x, z_hi), pts: 16 (over z_lo, y, core).
Axes of the slice: x: 4, y: 4, z: 8 (z_hi: 4, z_lo: 2; z = z_hi * 2 + z_lo), core: 2. Of those that a mesh axis runs over, the one named last changes fastest.
Arguments:
- valence: bfloat16 [16, 32, 4096], P('ka', None, 'pts'), may hold values from -0.09375 to 0.09375
- conduction: bfloat16 [16, 32, 4096], P('ka', None, 'pts'), may hold values from -6 to 6
- trials: bfloat16 [16, 32, 256], P('ka'), may hold values from -6 to 6
- w_panels: bfloat16 [16, 4096, 4096], P('ka', 'pts'), may hold values from -0.109375 to 0.109375
- partner: int32 [3, 16], replicated, may hold values from 0 to 15, as said below
- owner: int32 [3], replicated, may hold values from 0 to 15, as said below
Outputs:
- applied: float32 [16, 32, 256], P('ka', None, 'pts')
The draws below stay inside these ranges and needn't reach their ends.
Inputs may be any that keep to these rules, and one draw needn't show every extreme that they name: For each q there is a displacement d with partner[q, k] = (k + d) mod 16 for every k; the 3 displacements differ, are not 0, and include 16 - 1 and 8. `owner`: the 3 entries differ.
All inputs are finite; a program needn't handle non-finite values.
Results may differ from the reference program's by a relative error of at most 0.005.
Values may be sent and summed in bfloat16 or wider, within the bound.
No kernel may reach another device: no remote copies, remote signals or barrier semaphores. Data moves between devices by JAX's collectives and lax.ppermute only.
A program may use at most 64 MiB of HBM per device.

```python
import math
import jax
import jax.numpy as jnp
from jax import lax

NV = 32
NC = 32
NMU = 4096
NQ = 3
TR = 8
K = 16


def draw_partner(key, part):
    pick = jax.random.randint(jax.random.fold_in(key, 11), (), 0, K - 3).astype(jnp.int32) + 1
    pick = pick + (pick >= K // 2).astype(jnp.int32)
    fixed_set = jnp.stack([pick, jnp.int32(K // 2), jnp.int32(K - 1)]).astype(jnp.int32)
    order = jax.random.permutation(jax.random.fold_in(key, 13), 3)
    offsets = fixed_set[order][:NQ]
    return ((jnp.arange(K, dtype=jnp.int32)[None, :] + offsets[:, None].astype(jnp.int32)) % K).astype(jnp.int32)


def draw_owner(key, part):
    middle = jax.random.randint(jax.random.fold_in(key, 23), (), 1, K - 1).astype(jnp.int32)
    slots = jnp.stack([jnp.int32(0), middle, jnp.int32(K - 1)]).astype(jnp.int32)
    order = jax.random.permutation(jax.random.fold_in(key, 29), 3)
    return slots[order][:NQ].astype(jnp.int32)


def shard_levels(own_key, shape, cuts, least, largest):
    def one(position, shards_of):
        heights = jax.random.uniform(jax.random.fold_in(jax.random.fold_in(own_key, 6), position), (shards_of,), jnp.float32, least / len(cuts), largest / len(cuts))
        return jnp.repeat(jnp.exp(heights), shape[position] // shards_of).reshape((-1,) + (1,) * (len(shape) - position - 1))

    factor_of = one(*cuts[0])
    for cut in cuts[1:]:
        factor_of = factor_of * one(*cut)
    return factor_of


def scatter_about(key, shape, scale, bound, pieces=(), kind=jnp.bfloat16):
    array = jax.random.normal(key, shape, jnp.float32) * scale
    if len(pieces) > 0:
        array = shard_levels(key, shape, pieces, -0.22, 0.18) * array
    return jnp.clip(array, min=-bound, max=bound).astype(kind)


def setup_inputs(seed: int = 0) -> dict:
    streams_of = jax.random.split(jax.random.key(seed), 7)
    return {
        "valence": scatter_about(streams_of[0], (K, NV, NMU), NMU ** -0.5, 0.09375, ((0, 16), (2, 16))),
        "conduction": scatter_about(streams_of[1], (K, NC, NMU), 1.0, 6.0, ((0, 16), (2, 16))),
        "trials": scatter_about(streams_of[2], (K, NV, NC * TR), 1.0, 6.0, ((0, 16),)),
        "w_panels": scatter_about(streams_of[3], (K, NMU, NMU), (3 * NV * NC) ** -0.5, 0.109375, ((0, 16), (1, 16))),
        "partner": draw_partner(jax.random.fold_in(streams_of[6], 71), 0),
        "owner": draw_owner(jax.random.fold_in(streams_of[6], 71), 0),
    }


def reference(valence, conduction, trials, w_panels, partner, owner):
    width = math.gcd(NMU, 512)
    nblocks = NMU // width

    def one_point(kidx):
        total = jnp.zeros((NV, NC, TR), jnp.float32)
        own_val = valence[kidx].astype(jnp.float32)
        own_cond = conduction[kidx].reshape(NC, nblocks, width).transpose(1, 0, 2)
        for q in range(NQ):
            other = partner[q, kidx]
            panel = w_panels[owner[q]].reshape(nblocks, width, NMU)
            far_val = valence[other].astype(jnp.float32)
            far_cond = conduction[other].astype(jnp.float32)
            far_trial = trials[other].reshape(NV, NC, TR).astype(jnp.float32)
            block = jnp.einsum("cm,vct->mvt", far_cond, far_trial).astype(jnp.bfloat16)
            block = block.reshape(nblocks, width, NV, TR)

            def one_block(items):
                piece, rows, cond_rows = items
                image = jnp.einsum("mvt,vn->mnt", piece.astype(jnp.float32), far_val)
                weighted = (rows.astype(jnp.float32)[:, :, None] * image).astype(jnp.bfloat16)
                back = jnp.einsum("mnt,wn->mwt", weighted.astype(jnp.float32), own_val)
                return jnp.einsum("cm,mwt->wct", cond_rows.astype(jnp.float32), back)

            total = total + jnp.sum(lax.map(one_block, (block, panel, own_cond)), axis=0)
        return total.reshape(NV, NC * TR)

    return lax.map(one_point, jnp.arange(K, dtype=jnp.int32))
```

```python
import jax
import jax.numpy as jnp
from jax import lax
from jax.experimental import pallas as pl
from jax.experimental.pallas import tpu as pltpu
from jax.sharding import PartitionSpec as P


F32 = jnp.float32
BF16 = jnp.bfloat16
AXES = ("ka", "pts")


def coords(i):
    return [i // 64, (i // 16) % 4, (i // 8) % 2, (i // 2) % 4, i % 2]


def linear(v):
    return (((v[0] * 4 + v[1]) * 2 + v[2]) * 4 + v[3]) * 2 + v[4]


def move(a, f):
    pairs = []
    for i in range(256):
        v = coords(i)
        pairs.append((i, linear(f(v))))
    return lax.ppermute(a, AXES, pairs)


def flip(a, dim, mask):
    def f(v):
        w = list(v)
        w[dim] ^= mask if dim in (2, 4) or v[4] == 0 else 4 - mask
        return w

    return move(a, f)


def gray(s):
    return s ^ (s >> 1)


def half_pos(s):
    return 2 * ((s ^ (s >> 1)) & 1) + (s >> 1)


def pos_gather(s, c):
    return jnp.where(c == 0, gray(s), half_pos(s))


def pos_reduce(s, c):
    return jnp.where(c == 0, half_pos(s), gray(s))


def double(a, dim, mask):
    return jnp.concatenate([a, flip(a, dim, mask)], axis=0)


def cut_kernel(meta, w, o0, o1, o2, o3, sems):
    x = meta[0]
    copies = []
    for d, o in enumerate((o0, o1, o2, o3)):
        at = (x + d) & 3
        for zs in range(2):
            src = w.at[0, :, pl.ds(pl.multiple_of(zs * 2048 + at * 512, 512), 512)]
            dst = o.at[:, zs * 512 : zs * 512 + 512]
            copies.append(pltpu.make_async_copy(src, dst, sems.at[d * 2 + zs]))
    for cp in copies:
        cp.start()
    for cp in copies:
        cp.wait()


def cut(meta, w):
    hbm = pl.BlockSpec(memory_space=pl.ANY)
    vm = pl.BlockSpec(memory_space=pltpu.VMEM)
    return pl.pallas_call(
        cut_kernel,
        out_shape=[jax.ShapeDtypeStruct((256, 1024), BF16)] * 4,
        in_specs=[pl.BlockSpec(memory_space=pltpu.SMEM), hbm],
        out_specs=[vm] * 4,
        scratch_shapes=[pltpu.SemaphoreType.DMA((8,))],
        name="cut",
    )(meta, w)


def kernel(meta, w0, w1, w2, w3, va, vb, ct, out, send, vf, blk, back, da, db, ga, gb, wt):
    x, zh, zl, y, c = meta[0], meta[1], meta[2], meta[3], meta[4]

    def place(k, own, far):
        kx, kz = k // 4, k % 4
        py = pos_gather(kx ^ y, c)
        pz = pos_gather(kz ^ zh, c)
        far_py = pos_gather(kx ^ y, 1 - c)
        far_pz = pos_gather(kz ^ zh, 1 - c)
        for zs in range(2):
            rz = zs ^ zl
            here = (py * 2 + rz) * 4 + pz
            there = (far_py * 2 + rz) * 4 + far_pz
            for cs in range(2):
                src = (own, far)[cs]
                yield zs, cs, src, jnp.where(c == cs, here, there)

    def spread(first, second):
        def body(k, _):
            for zs, cs, src, idx in place(k, first, second):
                col = (zs * 2 + cs) * 256
                vf[k, :, col : col + 256] = src[idx].astype(F32)
            return 0

        lax.fori_loop(0, 16, body, 0)

    def slot_active(q):
        return (meta[8 + q] % 4) == zh

    any_active = slot_active(0) | slot_active(1) | slot_active(2)

    back[...] = jnp.zeros_like(back)

    @pl.when(any_active)
    def _():
        pl.when(c == 0)(lambda: spread(va, vb))
        pl.when(c == 1)(lambda: spread(vb, va))

        lane = lax.broadcasted_iota(jnp.int32, (32, 8, 256), 2)
        row = lax.broadcasted_iota(jnp.int32, (32, 8, 256), 1)
        same = (lane & 7) == row

        def blocks(k, _):
            kx, kz = k // 4, k % 4
            idx = pos_gather(kz ^ zh, c) * 9 + pos_gather(kx ^ x, c) * 2
            cond = ct[idx].astype(F32)
            tri = ct[idx + 1].astype(F32)
            lhs = jnp.where(same, tri[:, None, :], 0.0).reshape(256, 256).astype(BF16)
            rhs = jnp.broadcast_to(cond[:, None, :], (32, 8, 256)).reshape(256, 256).astype(BF16)
            got = lax.dot_general(lhs, rhs, (((1,), (0,)), ((), ())), preferred_element_type=F32)
            blk[k] = got.astype(BF16).astype(F32)
            return 0

        lax.fori_loop(0, 16, blocks, 0)

    def build(dref, k, p, g):
        own = vf[k]
        for i in range(16):
            line = vf[p, pl.ds(g * 16 + i, 1), :]
            dref[i * 32 : (i + 1) * 32, :] = (own * line).astype(BF16)

    def multiply(gref, dref):
        gref[...] = lax.dot_general(
            dref[...], wt[...], (((1,), (0,)), ((), ())), preferred_element_type=F32
        )

    def contract(gref, k, p, g):
        for s in range(4):
            acc = [back[k, t * 32 + s * 8 : t * 32 + s * 8 + 8, :] for t in range(8)]
            for i in range(16):
                val = gref[i * 32 + s * 8 : i * 32 + s * 8 + 8, :]
                for t in range(8):
                    acc[t] = acc[t] + blk[p, (g * 16 + i) * 8 + t : (g * 16 + i) * 8 + t + 1, :] * val
            for t in range(8):
                back[k, t * 32 + s * 8 : t * 32 + s * 8 + 8, :] = acc[t]

    def one(q, _):
        @pl.when(slot_active(q))
        def _():
            d = (x - meta[8 + q] // 4) & 3
            for j, w in enumerate((w0, w1, w2, w3)):

                def turn(w=w):
                    wt[...] = w[...].T

                pl.when(d == j)(turn)
            db[...] = jnp.zeros_like(db)
            ga[...] = jnp.zeros_like(ga)

            def body(k, _):
                kc = jnp.minimum(k, 15)
                pc = meta[16 + q * 16 + kc]
                ko = jnp.maximum(k - 1, 0)
                po = meta[16 + q * 16 + ko]
                multiply(gb, db)
                build(da, kc, pc, 0)
                contract(ga, ko, po, 0)
                multiply(ga, da)
                build(db, kc, pc, 1)
                contract(gb, ko, po, 1)
                return 0

            lax.fori_loop(0, 17, body, 0)

        return 0

    lax.fori_loop(0, 3, one, 0)

    r = lax.broadcasted_iota(jnp.int32, (32, 32), 0)
    col = lax.broadcasted_iota(jnp.int32, (32, 32), 1)
    ry = (r >> 2) & 3
    even = jnp.where(ry == 0, 0, jnp.where(ry == 1, 3, ry - 1))
    ys = jnp.where(((r >> 4) ^ c) == 0, even, ry ^ (ry >> 1))
    want = ((((r >> 1) & 1) ^ zl) * 4 + (ys ^ y)) * 4 + ((r >> 4) ^ c) * 2 + (r & 1)
    pick = jnp.where(col == want, 1.0, 0.0).astype(BF16)

    def last(k, _):
        kx, kz = k // 4, k % 4
        idx = pos_gather(kz ^ zh, c) * 9 + pos_gather(kx ^ x, c) * 2
        cond = lax.dot_general(
            pick, ct[idx], (((1,), (0,)), ((), ())), preferred_element_type=F32
        ).astype(BF16)
        b = back[k]
        hi = b.astype(BF16)
        lo = (b - hi.astype(F32)).astype(BF16)
        nt = (((1,), (1,)), ((), ()))
        res = lax.dot_general(cond, hi, nt, preferred_element_type=F32)
        res = res + lax.dot_general(cond, lo, nt, preferred_element_type=F32)
        at = pos_reduce(kx ^ x, c) * 4 + pos_reduce(kz ^ zh, c)
        out[at] = res[:16]
        far = pos_reduce(kx ^ x, 1 - c) * 4 + pos_reduce(kz ^ zh, 1 - c)
        send[far] = res[16:].astype(BF16)
        return 0

    lax.fori_loop(0, 16, last, 0)


def local(meta, w0, w1, w2, w3, va, vb, ct):
    vm = pl.BlockSpec(memory_space=pltpu.VMEM)
    return pl.pallas_call(
        kernel,
        out_shape=[
            jax.ShapeDtypeStruct((16, 16, 256), F32),
            jax.ShapeDtypeStruct((16, 16, 256), BF16),
        ],
        in_specs=[pl.BlockSpec(memory_space=pltpu.SMEM)] + [vm] * 7,
        out_specs=[vm, vm],
        scratch_shapes=[
            pltpu.VMEM((16, 32, 1024), F32),
            pltpu.VMEM((16, 256, 256), F32),
            pltpu.VMEM((16, 256, 256), F32),
            pltpu.VMEM((512, 1024), BF16),
            pltpu.VMEM((512, 1024), BF16),
            pltpu.VMEM((512, 256), F32),
            pltpu.VMEM((512, 256), F32),
            pltpu.VMEM((1024, 256), BF16),
        ],
        compiler_params=pltpu.CompilerParams(vmem_limit_bytes=48 << 20),
        name="screened",
    )(meta, w0, w1, w2, w3, va, vb, ct)


def steps(valence, conduction, trials, w_panels, partner, owner):
    ka = lax.axis_index("ka")
    pts = lax.axis_index("pts")
    x, zh = ka // 4, ka % 4
    zl, y, c = pts // 8, (pts // 2) % 4, pts % 2
    spot = jnp.arange(16, dtype=jnp.int32)
    place = jnp.where(spot == 0, x, jnp.where(spot == 1, zh, jnp.where(spot == 2, zl, jnp.where(spot == 3, y, c))))
    place = place.astype(jnp.int32)
    meta = jnp.concatenate([place[:8], owner, place[11:], partner.reshape(-1)])

    got = list(cut(place, w_panels))
    for d in (1, 2, 3):

        def shift(v, d=d):
            return [(v[0] + d) % 4] + v[1:]

        got[d] = move(got[d], shift)

    ct = jnp.stack([conduction[0], trials[0]])[None]
    ct = double(ct, 0, 1)

    def swap(v):
        return [v[3], v[1], v[2], v[0], v[4]]

    va = move(valence, swap)

    ct = double(ct, 0, 3)
    ct = jnp.concatenate([ct.reshape(8, 32, 256), va], axis=0)
    ct = double(ct, 1, 1)
    ct = double(ct, 1, 3)
    va = ct[8::9]
    va = double(va, 2, 1)
    va = double(va, 3, 1)
    va = double(va, 3, 3)
    vb = flip(va, 4, 1)

    part, send = local(meta, *got, va, vb, ct)

    part = part + flip(send, 4, 1).astype(F32)
    part = part[:, :8] + flip(part[:, 8:].astype(BF16), 3, 1).astype(F32)
    part = part[:, :4] + flip(part[:, 4:].astype(BF16), 3, 3).astype(F32)
    part = part[:8] + flip(part[8:], 0, 1)
    part = part[:4] + flip(part[4:], 0, 3)
    part = part[:, :2] + flip(part[:, 2:], 2, 1)
    part = part[:2] + flip(part[2:], 1, 1)
    part = part[:1] + flip(part[1:], 1, 3)
    return part.reshape(2, 8, 32).transpose(2, 0, 1).reshape(1, 32, 16)


def solution(mesh):
    placed = (
        P("ka", None, "pts"),
        P("ka", None, "pts"),
        P("ka", None, None),
        P("ka", "pts", None),
        P(),
        P(),
    )
    return jax.shard_map(
        steps, mesh=mesh, in_specs=placed, out_specs=P("ka", None, "pts"), check_vma=False
    )
```

```python
import jax
import jax.numpy as jnp
from jax import lax
from jax.experimental import pallas as pl
from jax.experimental.pallas import tpu as pltpu
from jax.sharding import PartitionSpec as P


F32 = jnp.float32
BF16 = jnp.bfloat16
AXES = ("ka", "pts")


def coords(i):
    return [i // 64, (i // 16) % 4, (i // 8) % 2, (i // 2) % 4, i % 2]


def linear(v):
    return (((v[0] * 4 + v[1]) * 2 + v[2]) * 4 + v[3]) * 2 + v[4]


def move(a, f):
    pairs = []
    for i in range(256):
        v = coords(i)
        pairs.append((i, linear(f(v))))
    return lax.ppermute(a, AXES, pairs)


def flip(a, dim, mask):
    def f(v):
        w = list(v)
        w[dim] ^= mask if dim in (2, 4) or v[4] == 0 else 4 - mask
        return w

    return move(a, f)


def gray(s):
    return s ^ (s >> 1)


def half_pos(s):
    return 2 * ((s ^ (s >> 1)) & 1) + (s >> 1)


def pos_gather(s, c):
    return jnp.where(c == 0, gray(s), half_pos(s))


def pos_reduce(s, c):
    return jnp.where(c == 0, half_pos(s), gray(s))


def double(a, dim, mask):
    return jnp.concatenate([a, flip(a, dim, mask)], axis=0)


def cut_kernel(meta, w, o1, o2, o3, sems):
    x = meta[0]
    copies = []
    for d, o in enumerate((o1, o2, o3)):
        at = (x + d + 1) & 3
        for zs in range(2):
            src = w.at[0, :, pl.ds(pl.multiple_of(zs * 2048 + at * 512, 512), 512)]
            dst = o.at[:, zs * 512 : zs * 512 + 512]
            copies.append(pltpu.make_async_copy(src, dst, sems.at[d * 2 + zs]))
    for cp in copies:
        cp.start()
    for cp in copies:
        cp.wait()


def cut(meta, w):
    hbm = pl.BlockSpec(memory_space=pl.ANY)
    vm = pl.BlockSpec(memory_space=pltpu.VMEM)
    return pl.pallas_call(
        cut_kernel,
        out_shape=[jax.ShapeDtypeStruct((256, 1024), BF16)] * 3,
        in_specs=[pl.BlockSpec(memory_space=pltpu.SMEM), hbm],
        out_specs=[vm] * 3,
        scratch_shapes=[pltpu.SemaphoreType.DMA((6,))],
        name="cut",
    )(meta, w)


def kernel(meta, panel, w1, w2, w3, va, vb, out, send, vf, blk, back, da, db, ga, gb, wt, w0, sems):
    x, zh, zl, y, c = meta[0], meta[1], meta[2], meta[3], meta[4]

    def place(k, own, far):
        kx, kz = k // 4, k % 4
        py = pos_gather(kx ^ y, c)
        pz = pos_gather(kz ^ zh, c)
        far_py = pos_gather(kx ^ y, 1 - c)
        far_pz = pos_gather(kz ^ zh, 1 - c)
        for zs in range(2):
            rz = zs ^ zl
            here = pz * 16 + 8 + py * 2 + rz
            there = far_pz * 16 + 8 + far_py * 2 + rz
            for cs in range(2):
                src = (own, far)[cs]
                yield zs, cs, src, jnp.where(c == cs, here, there)

    def spread(first, second):
        def body(k, _):
            for zs, cs, src, idx in place(k, first, second):
                col = (zs * 2 + cs) * 256
                vf[k, :, col : col + 256] = src[idx].astype(F32)
            return 0

        lax.fori_loop(0, 16, body, 0, unroll=2)

    def slot_active(q):
        return (meta[8 + q] % 4) == zh

    any_active = slot_active(0) | slot_active(1) | slot_active(2)

    back[...] = jnp.zeros_like(back)

    @pl.when(any_active)
    def _():
        pl.when(c == 0)(lambda: spread(va, vb))
        pl.when(c == 1)(lambda: spread(vb, va))

        lane = lax.broadcasted_iota(jnp.int32, (32, 8, 256), 2)
        row = lax.broadcasted_iota(jnp.int32, (32, 8, 256), 1)
        same = (lane & 7) == row

        def blocks(k, _):
            kx, kz = k // 4, k % 4
            idx = pos_gather(kz ^ zh, c) * 16 + pos_gather(kx ^ x, c) * 2
            cond = va[idx].astype(F32)
            tri = va[idx + 1].astype(F32)
            lhs = jnp.where(same, tri[:, None, :], 0.0).reshape(256, 256).astype(BF16)
            rhs = jnp.broadcast_to(cond[:, None, :], (32, 8, 256)).reshape(256, 256).astype(BF16)
            got = lax.dot_general(lhs, rhs, (((1,), (0,)), ((), ())), preferred_element_type=F32)
            blk[k] = got.astype(BF16).astype(F32)
            return 0

        lax.fori_loop(0, 16, blocks, 0, unroll=4)

    def build(dref, k, p, g):
        for j in range(4):
            ln = slice(j * 256, j * 256 + 256)
            own = vf[k, :, ln]
            for i in range(16):
                line = vf[p, g * 16 + i : g * 16 + i + 1, ln]
                dref[i * 32 : (i + 1) * 32, ln] = (own * line).astype(BF16)

    def multiply(gref, dref):
        gref[...] = lax.dot_general(
            dref[...], wt[...], (((1,), (0,)), ((), ())), preferred_element_type=F32
        )

    def contract2(k, p):
        for s in range(4):
            acc = [back[k, t * 32 + s * 8 : t * 32 + s * 8 + 8, :] for t in range(8)]
            for i in range(32):
                gref = ga if i < 16 else gb
                r = (i % 16) * 32 + s * 8
                val = gref[r : r + 8, :]
                for t in range(8):
                    acc[t] = acc[t] + blk[p, i * 8 + t : i * 8 + t + 1, :] * val
            for t in range(8):
                back[k, t * 32 + s * 8 : t * 32 + s * 8 + 8, :] = acc[t]

    def one(q, _):
        @pl.when(slot_active(q))
        def _():
            d = (x - meta[8 + q] // 4) & 3

            @pl.when(d == 0)
            def _():
                copies = []
                for zs in range(2):
                    src = panel.at[0, :, pl.ds(pl.multiple_of(zs * 2048 + x * 512, 512), 512)]
                    dst = w0.at[:, zs * 512 : zs * 512 + 512]
                    copies.append(pltpu.make_async_copy(src, dst, sems.at[zs]))
                for copy in copies:
                    copy.start()
                for copy in copies:
                    copy.wait()

            for j, w in enumerate((w0, w1, w2, w3)):

                def turn(w=w):
                    wt[...] = w[...].T

                pl.when(d == j)(turn)
            db[...] = jnp.zeros_like(db)
            ga[...] = jnp.zeros_like(ga)

            def body(k, _):
                kc = jnp.minimum(k, 15)
                pc = meta[16 + q * 16 + kc]
                ko = jnp.maximum(k - 1, 0)
                po = meta[16 + q * 16 + ko]
                multiply(gb, db)
                build(da, kc, pc, 0)
                build(db, kc, pc, 1)
                contract2(ko, po)
                multiply(ga, da)
                return 0

            lax.fori_loop(0, 17, body, 0)

        return 0

    lax.fori_loop(0, 3, one, 0)

    r = lax.broadcasted_iota(jnp.int32, (32, 32), 0)
    col = lax.broadcasted_iota(jnp.int32, (32, 32), 1)
    ry = (r >> 2) & 3
    even = jnp.where(ry == 0, 0, jnp.where(ry == 1, 3, ry - 1))
    ys = jnp.where(((r >> 4) ^ c) == 0, even, ry ^ (ry >> 1))
    want = ((((r >> 1) & 1) ^ zl) * 4 + (ys ^ y)) * 4 + ((r >> 4) ^ c) * 2 + (r & 1)
    pick = jnp.where(col == want, 1.0, 0.0).astype(BF16)

    def last(k, _):
        kx, kz = k // 4, k % 4
        idx = pos_gather(kz ^ zh, c) * 16 + pos_gather(kx ^ x, c) * 2
        cond = lax.dot_general(
            pick, va[idx], (((1,), (0,)), ((), ())), preferred_element_type=F32
        ).astype(BF16)
        b = back[k]
        hi = b.astype(BF16)
        lo = (b - hi.astype(F32)).astype(BF16)
        nt = (((1,), (1,)), ((), ()))
        res = lax.dot_general(cond, hi, nt, preferred_element_type=F32)
        res = res + lax.dot_general(cond, lo, nt, preferred_element_type=F32)
        at = pos_reduce(kx ^ x, c) * 4 + pos_reduce(kz ^ zh, c)
        out[at] = res[:16]
        far = pos_reduce(kx ^ x, 1 - c) * 4 + pos_reduce(kz ^ zh, 1 - c)
        send[far] = res[16:].astype(BF16)
        return 0

    lax.fori_loop(0, 16, last, 0, unroll=4)


def local(meta, panel, w1, w2, w3, va, vb):
    vm = pl.BlockSpec(memory_space=pltpu.VMEM)
    return pl.pallas_call(
        kernel,
        out_shape=[
            jax.ShapeDtypeStruct((16, 16, 256), F32),
            jax.ShapeDtypeStruct((16, 16, 256), BF16),
        ],
        in_specs=[pl.BlockSpec(memory_space=pltpu.SMEM), pl.BlockSpec(memory_space=pl.ANY)] + [vm] * 5,
        out_specs=[vm, vm],
        scratch_shapes=[
            pltpu.VMEM((16, 32, 1024), F32),
            pltpu.VMEM((16, 256, 256), F32),
            pltpu.VMEM((16, 256, 256), F32),
            pltpu.VMEM((512, 1024), BF16),
            pltpu.VMEM((512, 1024), BF16),
            pltpu.VMEM((512, 256), F32),
            pltpu.VMEM((512, 256), F32),
            pltpu.VMEM((1024, 256), BF16),
            pltpu.VMEM((256, 1024), BF16),
            pltpu.SemaphoreType.DMA((2,)),
        ],
        compiler_params=pltpu.CompilerParams(vmem_limit_bytes=48 << 20),
        name="screened",
    )(meta, panel, w1, w2, w3, va, vb)


def steps(valence, conduction, trials, w_panels, partner, owner):
    ka = lax.axis_index("ka")
    pts = lax.axis_index("pts")
    x, zh = ka // 4, ka % 4
    zl, y, c = pts // 8, (pts // 2) % 4, pts % 2
    spot = jnp.arange(16, dtype=jnp.int32)
    place = jnp.where(spot == 0, x, jnp.where(spot == 1, zh, jnp.where(spot == 2, zl, jnp.where(spot == 3, y, c))))
    place = place.astype(jnp.int32)
    meta = jnp.concatenate([place[:8], owner, place[11:], partner.reshape(-1)])

    got = list(cut(place, w_panels))
    for d in (1, 2, 3):

        def shift(v, d=d):
            return [(v[0] + d) % 4] + v[1:]

        got[d - 1] = move(got[d - 1], shift)

    def swap(v):
        return [v[3], v[1], v[2], v[0], v[4]]

    va = move(valence, swap)
    va = double(va, 2, 1)
    va = double(va, 3, 1)
    va = double(va, 3, 3)

    ct = jnp.stack([conduction[0], trials[0]])
    ct = double(ct, 0, 1)
    ct = double(ct, 0, 3)
    va = jnp.concatenate([ct, va], axis=0)
    va = double(va, 1, 1)
    va = double(va, 1, 3)
    vb = flip(va, 4, 1)

    part, send = local(meta, w_panels, *got, va, vb)

    part = part + flip(send, 4, 1).astype(F32)
    part = part[:, :8] + flip(part[:, 8:].astype(BF16), 3, 1).astype(F32)
    part = part[:, :4] + flip(part[:, 4:].astype(BF16), 3, 3).astype(F32)
    part = part[:8] + flip(part[8:], 0, 1)
    part = part[:4] + flip(part[4:], 0, 3)
    part = part[:, :2] + flip(part[:, 2:], 2, 1)
    part = part[:2] + flip(part[2:], 1, 1)
    part = part[:1] + flip(part[1:], 1, 3)
    return part.reshape(2, 8, 32).transpose(2, 0, 1).reshape(1, 32, 16)


def solution(mesh):
    placed = (
        P("ka", None, "pts"),
        P("ka", None, "pts"),
        P("ka", None, None),
        P("ka", "pts", None),
        P(),
        P(),
    )
    return jax.shard_map(
        steps, mesh=mesh, in_specs=placed, out_specs=P("ka", None, "pts"), check_vma=False
    )
```

```python
import jax
import jax.numpy as jnp
from jax import lax
from jax.experimental import pallas as pl
from jax.experimental.pallas import tpu as pltpu
from jax.sharding import PartitionSpec as P


F32 = jnp.float32
BF16 = jnp.bfloat16
AXES = ("ka", "pts")


def coords(i):
    return [i // 64, (i // 16) % 4, (i // 8) % 2, (i // 2) % 4, i % 2]


def linear(v):
    return (((v[0] * 4 + v[1]) * 2 + v[2]) * 4 + v[3]) * 2 + v[4]


def move(a, f):
    pairs = []
    for i in range(256):
        v = coords(i)
        pairs.append((i, linear(f(v))))
    return lax.ppermute(a, AXES, pairs)


def flip(a, dim, mask):
    def f(v):
        w = list(v)
        w[dim] ^= mask if dim in (2, 4) or v[4] == 0 else 4 - mask
        return w

    return move(a, f)


def gray(s):
    return s ^ (s >> 1)


def half_pos(s):
    return 2 * ((s ^ (s >> 1)) & 1) + (s >> 1)


def pos_gather(s, c):
    return jnp.where(c == 0, gray(s), half_pos(s))


def pos_reduce(s, c):
    return jnp.where(c == 0, half_pos(s), gray(s))


def double(a, dim, mask):
    return jnp.concatenate([a, flip(a, dim, mask)], axis=0)


def cut_kernel(meta, w, o1, o2, o3, sems):
    x = meta[0]
    copies = []
    for d, o in enumerate((o1, o2, o3)):
        at = (x + d + 1) & 3
        for zs in range(2):
            src = w.at[0, :, pl.ds(pl.multiple_of(zs * 2048 + at * 512, 512), 512)]
            dst = o.at[:, zs * 512 : zs * 512 + 512]
            copies.append(pltpu.make_async_copy(src, dst, sems.at[d * 2 + zs]))
    for cp in copies:
        cp.start()
    for cp in copies:
        cp.wait()


def cut(meta, w):
    hbm = pl.BlockSpec(memory_space=pl.ANY)
    vm = pl.BlockSpec(memory_space=pltpu.VMEM)
    return pl.pallas_call(
        cut_kernel,
        out_shape=[jax.ShapeDtypeStruct((256, 1024), BF16)] * 3,
        in_specs=[pl.BlockSpec(memory_space=pltpu.SMEM), hbm],
        out_specs=[vm] * 3,
        scratch_shapes=[pltpu.SemaphoreType.DMA((6,))],
        compiler_params=pltpu.CompilerParams(vmem_limit_bytes=4 << 20),
        name="cut",
    )(meta, w)


def kernel(meta, panel, w1, w2, w3, va, vb, out, send, vf, blk, back, da, db, ga, gb, wt, w0, sems):
    x, zh, zl, y, c = meta[0], meta[1], meta[2], meta[3], meta[4]

    def place(k, own, far):
        kx, kz = k // 4, k % 4
        py = pos_gather(kx ^ y, c)
        pz = pos_gather(kz ^ zh, c)
        far_py = pos_gather(kx ^ y, 1 - c)
        far_pz = pos_gather(kz ^ zh, 1 - c)
        for zs in range(2):
            rz = zs ^ zl
            here = pz * 28 + 12 + (py * 2 + rz) * 2
            there = far_pz * 28 + 12 + (far_py * 2 + rz) * 2
            for cs in range(2):
                src = (own, far)[cs]
                yield zs, cs, src, jnp.where(c == cs, here, there)

    def spread(first, second):
        def body(k, _):
            for zs, cs, src, idx in place(k, first, second):
                col = (zs * 2 + cs) * 256
                vf[k, :16, col : col + 256] = src[idx].astype(F32)
                vf[k, 16:, col : col + 256] = src[idx + 1].astype(F32)
            return 0

        lax.fori_loop(0, 16, body, 0, unroll=2)

    def slot_active(q):
        return (meta[8 + q] % 4) == zh

    any_active = slot_active(0) | slot_active(1) | slot_active(2)

    back[...] = jnp.zeros_like(back)

    @pl.when(any_active)
    def _():
        pl.when(c == 0)(lambda: spread(va, vb))
        pl.when(c == 1)(lambda: spread(vb, va))

        lane = lax.broadcasted_iota(jnp.int32, (32, 8, 256), 2)
        row = lax.broadcasted_iota(jnp.int32, (32, 8, 256), 1)
        same = (lane & 7) == row

        def blocks(k, _):
            kx, kz = k // 4, k % 4
            idx = pos_gather(kz ^ zh, c) * 28 + pos_gather(kx ^ x, c) * 3
            far = pos_gather(kz ^ zh, 1 - c) * 28 + pos_gather(kx ^ x, 1 - c) * 3
            cond = jnp.concatenate([va[idx], va[idx + 1]], axis=0).astype(F32)
            mine, other = va[idx + 2].astype(F32), vb[far + 2].astype(F32)
            low = jnp.where(c == 0, mine, other)
            high = jnp.where(c == 0, other, mine)
            tri = jnp.concatenate([low, high], axis=0)
            lhs = jnp.where(same, tri[:, None, :], 0.0).reshape(256, 256).astype(BF16)
            rhs = jnp.broadcast_to(cond[:, None, :], (32, 8, 256)).reshape(256, 256).astype(BF16)
            got = lax.dot_general(lhs, rhs, (((1,), (0,)), ((), ())), preferred_element_type=F32)
            blk[k] = got.astype(BF16).astype(F32)
            return 0

        lax.fori_loop(0, 16, blocks, 0, unroll=4)

    def build(dref, k, p, g):
        for j in range(4):
            ln = slice(j * 256, j * 256 + 256)
            own = vf[k, :, ln]
            for i in range(16):
                line = vf[p, g * 16 + i : g * 16 + i + 1, ln]
                dref[i * 32 : (i + 1) * 32, ln] = (own * line).astype(BF16)

    def multiply(gref, dref):
        gref[...] = lax.dot_general(
            dref[...], wt[...], (((1,), (0,)), ((), ())), preferred_element_type=F32
        )

    def contract2(k, p):
        for s in range(4):
            acc = [back[k, t * 32 + s * 8 : t * 32 + s * 8 + 8, :] for t in range(8)]
            for i in range(32):
                gref = ga if i < 16 else gb
                r = (i % 16) * 32 + s * 8
                val = gref[r : r + 8, :]
                for t in range(8):
                    acc[t] = acc[t] + blk[p, i * 8 + t : i * 8 + t + 1, :] * val
            for t in range(8):
                back[k, t * 32 + s * 8 : t * 32 + s * 8 + 8, :] = acc[t]

    def one(q, _):
        @pl.when(slot_active(q))
        def _():
            d = (x - meta[8 + q] // 4) & 3

            @pl.when(d == 0)
            def _():
                copies = []
                for zs in range(2):
                    src = panel.at[0, :, pl.ds(pl.multiple_of(zs * 2048 + x * 512, 512), 512)]
                    dst = w0.at[:, zs * 512 : zs * 512 + 512]
                    copies.append(pltpu.make_async_copy(src, dst, sems.at[zs]))
                for copy in copies:
                    copy.start()
                for copy in copies:
                    copy.wait()

            for j, w in enumerate((w0, w1, w2, w3)):

                def turn(w=w):
                    wt[...] = w[...].T

                pl.when(d == j)(turn)
            db[...] = jnp.zeros_like(db)
            ga[...] = jnp.zeros_like(ga)

            def body(k, _):
                kc = jnp.minimum(k, 15)
                pc = meta[16 + q * 16 + kc]
                ko = jnp.maximum(k - 1, 0)
                po = meta[16 + q * 16 + ko]
                multiply(gb, db)
                build(da, kc, pc, 0)
                build(db, kc, pc, 1)
                contract2(ko, po)
                multiply(ga, da)
                return 0

            lax.fori_loop(0, 17, body, 0)

        return 0

    lax.fori_loop(0, 3, one, 0)

    r = lax.broadcasted_iota(jnp.int32, (32, 32), 0)
    col = lax.broadcasted_iota(jnp.int32, (32, 32), 1)
    ry = (r >> 2) & 3
    even = jnp.where(ry == 0, 0, jnp.where(ry == 1, 3, ry - 1))
    ys = jnp.where(((r >> 4) ^ c) == 0, even, ry ^ (ry >> 1))
    want = ((((r >> 1) & 1) ^ zl) * 4 + (ys ^ y)) * 4 + ((r >> 4) ^ c) * 2 + (r & 1)
    pick = jnp.where(col == want, 1.0, 0.0).astype(BF16)

    def last(k, _):
        kx, kz = k // 4, k % 4
        idx = pos_gather(kz ^ zh, c) * 28 + pos_gather(kx ^ x, c) * 3
        both = jnp.concatenate([va[idx], va[idx + 1]], axis=0)
        cond = lax.dot_general(
            pick, both, (((1,), (0,)), ((), ())), preferred_element_type=F32
        ).astype(BF16)
        b = back[k]
        hi = b.astype(BF16)
        lo = (b - hi.astype(F32)).astype(BF16)
        nt = (((1,), (1,)), ((), ()))
        res = lax.dot_general(cond, hi, nt, preferred_element_type=F32)
        res = res + lax.dot_general(cond, lo, nt, preferred_element_type=F32)
        at = pos_reduce(kx ^ x, c) * 4 + pos_reduce(kz ^ zh, c)
        out[at] = res[:16]
        far = pos_reduce(kx ^ x, 1 - c) * 4 + pos_reduce(kz ^ zh, 1 - c)
        send[far] = res[16:].astype(BF16)
        return 0

    lax.fori_loop(0, 16, last, 0, unroll=4)


def local(meta, panel, w1, w2, w3, va, vb):
    vm = pl.BlockSpec(memory_space=pltpu.VMEM)
    return pl.pallas_call(
        kernel,
        out_shape=[
            jax.ShapeDtypeStruct((16, 16, 256), F32),
            jax.ShapeDtypeStruct((16, 16, 256), BF16),
        ],
        in_specs=[pl.BlockSpec(memory_space=pltpu.SMEM), pl.BlockSpec(memory_space=pl.ANY)] + [vm] * 5,
        out_specs=[vm, vm],
        scratch_shapes=[
            pltpu.VMEM((16, 32, 1024), F32),
            pltpu.VMEM((16, 256, 256), F32),
            pltpu.VMEM((16, 256, 256), F32),
            pltpu.VMEM((512, 1024), BF16),
            pltpu.VMEM((512, 1024), BF16),
            pltpu.VMEM((512, 256), F32),
            pltpu.VMEM((512, 256), F32),
            pltpu.VMEM((1024, 256), BF16),
            pltpu.VMEM((256, 1024), BF16),
            pltpu.SemaphoreType.DMA((2,)),
        ],
        compiler_params=pltpu.CompilerParams(vmem_limit_bytes=28 << 20),
        name="screened",
    )(meta, panel, w1, w2, w3, va, vb)


def steps(valence, conduction, trials, w_panels, partner, owner):
    ka = lax.axis_index("ka")
    pts = lax.axis_index("pts")
    x, zh = ka // 4, ka % 4
    zl, y, c = pts // 8, (pts // 2) % 4, pts % 2
    spot = jnp.arange(16, dtype=jnp.int32)
    place = jnp.where(spot == 0, x, jnp.where(spot == 1, zh, jnp.where(spot == 2, zl, jnp.where(spot == 3, y, c))))
    place = place.astype(jnp.int32)
    meta = jnp.concatenate([place[:8], owner, place[11:], partner.reshape(-1)])

    got = list(cut(place, w_panels))
    for d in (1, 2, 3):

        def shift(v, d=d):
            return [(v[0] + d) % 4] + v[1:]

        got[d - 1] = move(got[d - 1], shift)

    def swap(v):
        return [v[3], v[1], v[2], v[0], v[4]]

    va = move(valence, swap)
    va = double(va, 2, 1)
    va = double(va, 3, 1)
    va = double(va, 3, 3)

    half = lax.dynamic_slice_in_dim(trials[0], c * 16, 16, axis=0)
    ct = jnp.concatenate([conduction[0], half], axis=0).reshape(3, 16, 256)
    ct = double(ct, 0, 1)
    ct = double(ct, 0, 3)
    va = jnp.concatenate([ct, va.reshape(16, 16, 256)], axis=0)
    va = double(va, 1, 1)
    va = double(va, 1, 3)
    vb = flip(va, 4, 1)

    part, send = local(meta, w_panels, *got, va, vb)

    part = part + flip(send, 4, 1).astype(F32)
    part = part[:, :8] + flip(part[:, 8:].astype(BF16), 3, 1).astype(F32)
    part = part[:, :4] + flip(part[:, 4:].astype(BF16), 3, 3).astype(F32)
    part = part[:8] + flip(part[8:], 0, 1)
    part = part[:4] + flip(part[4:], 0, 3)
    part = part[:, :2] + flip(part[:, 2:], 2, 1)
    part = part[:2] + flip(part[2:], 1, 1)
    part = part[:1] + flip(part[1:], 1, 3)
    return part.reshape(2, 8, 32).transpose(2, 0, 1).reshape(1, 32, 16)


def solution(mesh):
    placed = (
        P("ka", None, "pts"),
        P("ka", None, "pts"),
        P("ka", None, None),
        P("ka", "pts", None),
        P(),
        P(),
    )
    return jax.shard_map(
        steps, mesh=mesh, in_specs=placed, out_specs=P("ka", None, "pts"), check_vma=False
    )
```

```python
import jax
import jax.numpy as jnp
from jax import lax
from jax.experimental import pallas as pl
from jax.experimental.pallas import tpu as pltpu
from jax.sharding import PartitionSpec as P


F32 = jnp.float32
BF16 = jnp.bfloat16
AXES = ("ka", "pts")


def coords(i):
    return [i // 64, (i // 16) % 4, (i // 8) % 2, (i // 2) % 4, i % 2]


def linear(v):
    return (((v[0] * 4 + v[1]) * 2 + v[2]) * 4 + v[3]) * 2 + v[4]


def move(a, f):
    pairs = []
    for i in range(256):
        v = coords(i)
        pairs.append((i, linear(f(v))))
    return lax.ppermute(a, AXES, pairs)


def flip(a, dim, mask):
    def f(v):
        w = list(v)
        w[dim] ^= mask if dim in (2, 4) or v[4] == 0 else 4 - mask
        return w

    return move(a, f)


def gray(s):
    return s ^ (s >> 1)


def half_pos(s):
    return 2 * ((s ^ (s >> 1)) & 1) + (s >> 1)


def pos_gather(s, c):
    return jnp.where(c == 0, gray(s), half_pos(s))


def pos_reduce(s, c):
    return jnp.where(c == 0, half_pos(s), gray(s))


def double(a, dim, mask):
    return jnp.concatenate([a, flip(a, dim, mask)], axis=0)


def cut_kernel(meta, w, o1, o2, o3, sems):
    x = meta[0]
    copies = []
    for d, o in enumerate((o1, o2, o3)):
        at = (x + d + 1) & 3
        for zs in range(2):
            src = w.at[0, :, pl.ds(pl.multiple_of(zs * 2048 + at * 512, 512), 512)]
            dst = o.at[:, zs * 512 : zs * 512 + 512]
            copies.append(pltpu.make_async_copy(src, dst, sems.at[d * 2 + zs]))
    for cp in copies:
        cp.start()
    for cp in copies:
        cp.wait()


def cut(meta, w):
    hbm = pl.BlockSpec(memory_space=pl.ANY)
    vm = pl.BlockSpec(memory_space=pltpu.VMEM)
    return pl.pallas_call(
        cut_kernel,
        out_shape=[jax.ShapeDtypeStruct((256, 1024), BF16)] * 3,
        in_specs=[pl.BlockSpec(memory_space=pltpu.SMEM), hbm],
        out_specs=[vm] * 3,
        scratch_shapes=[pltpu.SemaphoreType.DMA((6,))],
        name="cut",
    )(meta, w)


def kernel(meta, panel, w1, w2, w3, va, vb, out, send, vf, blk, back, da, db, ga, gb, wt, w0, sems):
    x, zh, zl, y, c = meta[0], meta[1], meta[2], meta[3], meta[4]

    def place(k, own, far):
        kx, kz = k // 4, k % 4
        py = pos_gather(kx ^ y, c)
        pz = pos_gather(kz ^ zh, c)
        far_py = pos_gather(kx ^ y, 1 - c)
        far_pz = pos_gather(kz ^ zh, 1 - c)
        for zs in range(2):
            rz = zs ^ zl
            here = pz * 16 + 8 + py * 2 + rz
            there = far_pz * 16 + 8 + far_py * 2 + rz
            for cs in range(2):
                src = (own, far)[cs]
                yield zs, cs, src, jnp.where(c == cs, here, there)

    def spread(first, second):
        def body(k, _):
            for zs, cs, src, idx in place(k, first, second):
                col = (zs * 2 + cs) * 256
                vf[k, :, col : col + 256] = src[idx].astype(F32)
            return 0

        lax.fori_loop(0, 16, body, 0, unroll=2)

    def slot_active(q):
        return (meta[8 + q] % 4) == zh

    any_active = slot_active(0) | slot_active(1) | slot_active(2)

    back[...] = jnp.zeros_like(back)

    @pl.when(any_active)
    def _():
        pl.when(c == 0)(lambda: spread(va, vb))
        pl.when(c == 1)(lambda: spread(vb, va))

        lane = lax.broadcasted_iota(jnp.int32, (32, 8, 256), 2)
        row = lax.broadcasted_iota(jnp.int32, (32, 8, 256), 1)
        same = (lane & 7) == row

        def blocks(k, _):
            kx, kz = k // 4, k % 4
            idx = pos_gather(kz ^ zh, c) * 16 + pos_gather(kx ^ x, c) * 2
            cond = va[idx].astype(F32)
            tri = va[idx + 1].astype(F32)
            lhs = jnp.where(same, tri[:, None, :], 0.0).reshape(256, 256).astype(BF16)
            rhs = jnp.broadcast_to(cond[:, None, :], (32, 8, 256)).reshape(256, 256).astype(BF16)
            got = lax.dot_general(lhs, rhs, (((1,), (0,)), ((), ())), preferred_element_type=F32)
            blk[k] = got.astype(BF16).astype(F32)
            return 0

        lax.fori_loop(0, 16, blocks, 0, unroll=4)

    def build(dref, k, p, g):
        for j in range(4):
            ln = slice(j * 256, j * 256 + 256)
            own = vf[k, :, ln]
            for i in range(16):
                line = vf[p, g * 16 + i : g * 16 + i + 1, ln]
                dref[i * 32 : (i + 1) * 32, ln] = (own * line).astype(BF16)

    def multiply(gref, dref):
        gref[...] = lax.dot_general(
            dref[...], wt[...], (((1,), (0,)), ((), ())), preferred_element_type=F32
        )

    def contract2(k, p):
        for s in range(4):
            acc = [back[k, t * 32 + s * 8 : t * 32 + s * 8 + 8, :] for t in range(8)]
            for i in range(32):
                gref = ga if i < 16 else gb
                r = (i % 16) * 32 + s * 8
                val = gref[r : r + 8, :]
                for t in range(8):
                    acc[t] = acc[t] + blk[p, i * 8 + t : i * 8 + t + 1, :] * val
            for t in range(8):
                back[k, t * 32 + s * 8 : t * 32 + s * 8 + 8, :] = acc[t]

    def one(q, _):
        @pl.when(slot_active(q))
        def _():
            d = (x - meta[8 + q] // 4) & 3

            @pl.when(d == 0)
            def _():
                copies = []
                for zs in range(2):
                    src = panel.at[0, :, pl.ds(pl.multiple_of(zs * 2048 + x * 512, 512), 512)]
                    dst = w0.at[:, zs * 512 : zs * 512 + 512]
                    copies.append(pltpu.make_async_copy(src, dst, sems.at[zs]))
                for copy in copies:
                    copy.start()
                for copy in copies:
                    copy.wait()

            for j, w in enumerate((w0, w1, w2, w3)):

                def turn(w=w):
                    wt[...] = w[...].T

                pl.when(d == j)(turn)

            def mate(k):
                return meta[16 + q * 16 + k]

            build(da, 0, mate(0), 0)
            build(db, 0, mate(0), 1)
            multiply(ga, da)

            def body(k, _):
                multiply(gb, db)
                build(da, k, mate(k), 0)
                build(db, k, mate(k), 1)
                contract2(k - 1, mate(k - 1))
                multiply(ga, da)
                return 0

            lax.fori_loop(1, 16, body, 0)
            multiply(gb, db)
            contract2(15, mate(15))

        return 0

    lax.fori_loop(0, 3, one, 0)

    r = lax.broadcasted_iota(jnp.int32, (32, 32), 0)
    col = lax.broadcasted_iota(jnp.int32, (32, 32), 1)
    ry = (r >> 2) & 3
    even = jnp.where(ry == 0, 0, jnp.where(ry == 1, 3, ry - 1))
    ys = jnp.where(((r >> 4) ^ c) == 0, even, ry ^ (ry >> 1))
    want = ((((r >> 1) & 1) ^ zl) * 4 + (ys ^ y)) * 4 + ((r >> 4) ^ c) * 2 + (r & 1)
    pick = jnp.where(col == want, 1.0, 0.0).astype(BF16)

    def last(k, _):
        kx, kz = k // 4, k % 4
        idx = pos_gather(kz ^ zh, c) * 16 + pos_gather(kx ^ x, c) * 2
        cond = lax.dot_general(
            pick, va[idx], (((1,), (0,)), ((), ())), preferred_element_type=F32
        ).astype(BF16)
        b = back[k]
        hi = b.astype(BF16)
        lo = (b - hi.astype(F32)).astype(BF16)
        nt = (((1,), (1,)), ((), ()))
        res = lax.dot_general(cond, hi, nt, preferred_element_type=F32)
        res = res + lax.dot_general(cond, lo, nt, preferred_element_type=F32)
        at = pos_reduce(kx ^ x, c) * 4 + pos_reduce(kz ^ zh, c)
        out[at] = res[:16]
        far = pos_reduce(kx ^ x, 1 - c) * 4 + pos_reduce(kz ^ zh, 1 - c)
        send[far] = res[16:].astype(BF16)
        return 0

    lax.fori_loop(0, 16, last, 0, unroll=4)


def local(meta, panel, w1, w2, w3, va, vb):
    vm = pl.BlockSpec(memory_space=pltpu.VMEM)
    return pl.pallas_call(
        kernel,
        out_shape=[
            jax.ShapeDtypeStruct((16, 16, 256), F32),
            jax.ShapeDtypeStruct((16, 16, 256), BF16),
        ],
        in_specs=[pl.BlockSpec(memory_space=pltpu.SMEM), pl.BlockSpec(memory_space=pl.ANY)] + [vm] * 5,
        out_specs=[vm, vm],
        scratch_shapes=[
            pltpu.VMEM((16, 32, 1024), F32),
            pltpu.VMEM((16, 256, 256), F32),
            pltpu.VMEM((16, 256, 256), F32),
            pltpu.VMEM((512, 1024), BF16),
            pltpu.VMEM((512, 1024), BF16),
            pltpu.VMEM((512, 256), F32),
            pltpu.VMEM((512, 256), F32),
            pltpu.VMEM((1024, 256), BF16),
            pltpu.VMEM((256, 1024), BF16),
            pltpu.SemaphoreType.DMA((2,)),
        ],
        compiler_params=pltpu.CompilerParams(vmem_limit_bytes=48 << 20),
        name="screened",
    )(meta, panel, w1, w2, w3, va, vb)


def steps(valence, conduction, trials, w_panels, partner, owner):
    ka = lax.axis_index("ka")
    pts = lax.axis_index("pts")
    x, zh = ka // 4, ka % 4
    zl, y, c = pts // 8, (pts // 2) % 4, pts % 2
    spot = jnp.arange(16, dtype=jnp.int32)
    place = jnp.where(spot == 0, x, jnp.where(spot == 1, zh, jnp.where(spot == 2, zl, jnp.where(spot == 3, y, c))))
    place = place.astype(jnp.int32)
    meta = jnp.concatenate([place[:8], owner, place[11:], partner.reshape(-1)])

    got = list(cut(place, w_panels))
    for d in (1, 2, 3):

        def shift(v, d=d):
            return [(v[0] + d) % 4] + v[1:]

        got[d - 1] = move(got[d - 1], shift)

    def swap(v):
        return [v[3], v[1], v[2], v[0], v[4]]

    va = move(valence, swap)
    va = double(va, 2, 1)
    va = double(va, 3, 1)
    va = double(va, 3, 3)

    ct = jnp.stack([conduction[0], trials[0]])
    ct = double(ct, 0, 1)
    ct = double(ct, 0, 3)
    va = jnp.concatenate([ct, va], axis=0)
    va = double(va, 1, 1)
    va = double(va, 1, 3)
    vb = flip(va, 4, 1)

    part, send = local(meta, w_panels, *got, va, vb)

    part = part + flip(send, 4, 1).astype(F32)
    part = part[:, :8] + flip(part[:, 8:].astype(BF16), 3, 1).astype(F32)
    part = part[:, :4] + flip(part[:, 4:].astype(BF16), 3, 3).astype(F32)
    part = part[:8] + flip(part[8:], 0, 1)
    part = part[:4] + flip(part[4:], 0, 3)
    part = part[:, :2] + flip(part[:, 2:], 2, 1)
    part = part[:2] + flip(part[2:], 1, 1)
    part = part[:1] + flip(part[1:], 1, 3)
    return part.reshape(2, 8, 32).transpose(2, 0, 1).reshape(1, 32, 16)


def solution(mesh):
    placed = (
        P("ka", None, "pts"),
        P("ka", None, "pts"),
        P("ka", None, None),
        P("ka", "pts", None),
        P(),
        P(),
    )
    return jax.shard_map(
        steps, mesh=mesh, in_specs=placed, out_specs=P("ka", None, "pts"), check_vma=False
    )
```
